32 devices in a mesh: outer: 4 (over y, x), inner: 8 (over z, core).
Axes of the slice: x: 2, y: 2, z: 4, core: 2. Of those that a mesh axis runs over, the one named last changes fastest.
Arguments:
- p_factor: bfloat16 [56, 56, 16384], P('outer', None, 'inner'), may hold values from -24 to 24
- q_factor: bfloat16 [56, 56, 16384], P(None, None, 'inner'), may hold values from -6 to 6
- truncation: bfloat16 [3136, 56], P('outer'), may hold values from -0.109375 to 0.109375
Outputs:
- gram: float32 [3136, 3136], P('outer', 'inner')
- coarse: float32 [56, 16384], P(None, 'inner')
The draws below stay inside these ranges and needn't reach their ends.
All inputs are finite; a program needn't handle non-finite values.
Results may differ from the reference program's by a relative error of at most 0.003.
Values may be sent and summed in bfloat16 or wider, within the bound.
No kernel may reach another device: no remote copies, remote signals or barrier semaphores. Data moves between devices by JAX's collectives and lax.ppermute only.
A program may use at most 128 MiB of HBM per device.

```python
import math
import jax
import jax.numpy as jnp
from jax import lax

D = 56
M = 56
CDEV = 2048
DD = 3136
COLS = 16384


def draw_p_factor(key, part):
    first, second = jax.random.split(jax.random.fold_in(key, 17))
    base = jax.random.normal(first, (D, M, COLS), jnp.float32)
    position = jnp.arange(COLS, dtype=jnp.float32) / max(COLS - 1, 1)
    rising = 1.0 + 2.0 * position
    rough = jnp.exp(jax.random.uniform(second, (COLS,), jnp.float32, 0.0, math.log(3.0)))
    return jnp.clip(base * (rising * rough)[None, None, :], -24.0, 24.0).astype(jnp.bfloat16)


def steps_of(rng, extent, pieces, low, top_value):
    loudness = 1.0
    for dim, blocks in pieces:
        steps = jax.random.uniform(jax.random.fold_in(jax.random.fold_in(rng, 6), dim), (blocks,), jnp.float32, low / len(pieces), top_value / len(pieces))
        loudness = loudness * jnp.repeat(jnp.exp(steps), extent[dim] // blocks).reshape((-1,) + (1,) * (len(extent) - 1 - dim))
    return loudness


def bell_draw(rng, dims, scale, limit, cuts=(), kind=jnp.bfloat16):
    factor_of = steps_of(rng, dims, cuts, -0.22, 0.18) if cuts else 1.0
    array = jax.random.normal(rng, dims, jnp.float32) * scale * factor_of
    return jnp.minimum(jnp.maximum(array, -limit), limit).astype(kind)


def setup_inputs(seed: int = 0) -> dict:
    keys = jax.random.split(jax.random.key(seed), 4)
    p_factor = draw_p_factor(jax.random.fold_in(keys[3], 71), 0)
    q_factor = bell_draw(keys[1], (D, M, COLS), 1.0, 6.0, ((2, 8),))
    truncation = bell_draw(keys[2], (DD, D), DD ** -0.5, 0.109375, ((0, 4),))
    return dict(p_factor=p_factor, q_factor=q_factor, truncation=truncation)


def reference(p_factor, q_factor, truncation):
    count = COLS // CDEV

    def per_block(running, index_block):
        start = (index_block * CDEV).astype(jnp.int32)
        p_block = lax.dynamic_slice_in_dim(p_factor, start, CDEV, 2).astype(jnp.float32)
        q_block = lax.dynamic_slice_in_dim(q_factor, start, CDEV, 2).astype(jnp.float32)
        paired = jnp.einsum('imc,jmc->ijc', p_block, q_block) / math.sqrt(M)
        block_rows = paired.reshape(D * D, CDEV).astype(jnp.bfloat16)
        gram_term = lax.dot_general(block_rows, block_rows, (((1,), (1,)), ((), ())), preferred_element_type=jnp.float32)
        absorb_term = lax.dot_general(truncation, block_rows, (((0,), (0,)), ((), ())), preferred_element_type=jnp.float32)
        return (running + gram_term, absorb_term)
    start_gram = jnp.zeros((D * D, D * D), jnp.float32)
    summed, stacked = lax.scan(per_block, start_gram, jnp.arange(count, dtype=jnp.int32))
    gram = summed / COLS
    absorbed = jnp.transpose(stacked, (1, 0, 2)).reshape(D, COLS)
    norm_scale = jnp.sqrt(jnp.mean(absorbed * absorbed) + 1e-06)
    return (gram, absorbed / norm_scale)
```

```python
import functools
import math

import jax
import jax.numpy as jnp
from jax import lax
from jax.experimental import pallas as pl
from jax.experimental.pallas import tpu as pltpu
from jax.sharding import PartitionSpec as P

F32 = jnp.float32
BF16 = jnp.bfloat16
AXES = ("outer", "inner")
VMEM_LIMIT = 56 << 20
COLUMN_TILE = 256


def product_rows(p_ref, q_ref, rows, cols, scale, store):
    bond = q_ref.shape[0]

    def step(group, carry):
        base = pl.multiple_of(group * 8, 8)
        q_rows = [q_ref[base + u, :, cols].astype(F32) for u in range(8)]
        for half, i in rows:
            p_row = p_ref[half, i, :, cols].astype(F32)
            sums = [jnp.sum(p_row * q_row, axis=0, keepdims=True) for q_row in q_rows]
            store(half, i, base, (jnp.concatenate(sums, axis=0) * scale).astype(BF16))
        return carry

    lax.fori_loop(0, bond // 8, step, 0)


def first_kernel(lo, hi, scale, p_ref, q_ref, left_ref, right_ref):
    column = pl.program_id(0)
    bond = q_ref.shape[0]
    rows = [(h, i) for h in range(2) for i in range(lo, hi)]

    def run(out_ref):
        for c in range(0, p_ref.shape[3], 128):
            cols = slice(c, c + 128)

            def store(half, i, base, value):
                out_ref[half, pl.ds((i - lo) * bond + base, 8), cols] = value

            product_rows(p_ref, q_ref, rows, cols, scale, store)

    middle = pl.num_programs(0) // 2

    @pl.when(column < middle)
    def _():
        run(left_ref)

    @pl.when(column >= middle)
    def _():
        run(right_ref)


def contract_chunk(p4, q_factor, lo, hi):
    _, half_rows, bonds, columns = p4.shape
    bond = q_factor.shape[0]
    tile = COLUMN_TILE
    steps = columns // tile
    middle = steps // 2
    rows = (hi - lo) * bond
    scale = 1.0 / math.sqrt(bonds)
    out = jax.ShapeDtypeStruct((2, rows, columns // 2), BF16)
    return pl.pallas_call(
        functools.partial(first_kernel, lo, hi, scale),
        grid=(steps,),
        in_specs=[
            pl.BlockSpec((2, half_rows, bonds, tile), lambda c: (0, 0, 0, c)),
            pl.BlockSpec((bond, bonds, tile), lambda c: (0, 0, c)),
        ],
        out_specs=[
            pl.BlockSpec((2, rows, tile), lambda c: (0, 0, jnp.minimum(c, middle - 1))),
            pl.BlockSpec((2, rows, tile), lambda c: (0, 0, jnp.maximum(c - middle, 0))),
        ],
        out_shape=[out, out],
        compiler_params=pltpu.CompilerParams(vmem_limit_bytes=VMEM_LIMIT),
        cost_estimate=pl.CostEstimate(flops=60_000_000_000, bytes_accessed=16 << 20, transcendentals=0),
        name="contract",
    )(p4, q_factor)


def gram_kernel(core_ref, own0, own1, x0, x1, y0, y1, d0, d1, s_ref, keep_ref, send_ref):
    core = core_ref[0]
    half_cols = own0.shape[2]
    for k, (left, right) in enumerate(((own0, own1), (x0, x1), (y0, y1), (d0, d1))):
        for h in range(2):
            acc = lax.dot_general(
                left[h], s_ref[:, :half_cols], (((1,), (1,)), ((), ())), preferred_element_type=F32
            )
            acc += lax.dot_general(
                right[h], s_ref[:, half_cols:], (((1,), (1,)), ((), ())), preferred_element_type=F32
            )
            value = acc.astype(BF16)

            @pl.when(core == h)
            def _():
                keep_ref[k] = value

            @pl.when(core != h)
            def _():
                send_ref[k] = value


def gram_chunk(core, blocks, slab):
    rows = blocks[0].shape[1]
    total = slab.shape[0]
    out = jax.ShapeDtypeStruct((4, rows, total), BF16)
    vmem = pl.BlockSpec(memory_space=pltpu.VMEM)
    return pl.pallas_call(
        gram_kernel,
        in_specs=[pl.BlockSpec(memory_space=pltpu.SMEM)] + [vmem] * 9,
        out_specs=[vmem, vmem],
        out_shape=[out, out],
        compiler_params=pltpu.CompilerParams(vmem_limit_bytes=VMEM_LIMIT),
        cost_estimate=pl.CostEstimate(
            flops=2 * 8 * rows * total * slab.shape[1], bytes_accessed=12 << 20, transcendentals=0
        ),
        name="gram",
    )(core, *blocks, slab)


def merge_kernel(o_ref, keep_ref, recv_ref, out_ref):
    out_ref[...] = (keep_ref[...].astype(F32) + recv_ref[...].astype(F32)).astype(BF16)


def merge_chunk(outer_index, keep, recv):
    _, rows, total = keep.shape
    spec = pl.BlockSpec((1, rows, total), lambda d, o: (d ^ o[0], 0, 0))
    return pl.pallas_call(
        merge_kernel,
        grid_spec=pltpu.PrefetchScalarGridSpec(
            num_scalar_prefetch=1,
            grid=(4,),
            in_specs=[spec, spec],
            out_specs=pl.BlockSpec((1, rows, total), lambda d, o: (d, 0, 0)),
        ),
        out_shape=jax.ShapeDtypeStruct(keep.shape, BF16),
        name="merge",
    )(outer_index, keep, recv)


def pairs(target, keep):
    found = []
    for o in range(4):
        for z in range(4):
            for c in range(2):
                t = target(o, z, c)
                if keep(*t):
                    found.append((o * 8 + z * 2 + c, t[0] * 8 + t[1] * 2 + t[2]))
    return found


def move(value, target, keep=lambda o, z, c: True):
    return lax.ppermute(value, AXES, pairs(target, keep))


def low_rule(o, z, c):
    return (o & 1) == c


def high_rule(o, z, c):
    return (o >> 1) == c


def off_diagonal(o, z, c):
    return o != z


def to_x(o, z, c):
    return (o ^ 1, z, c)


def to_y(o, z, c):
    return (o ^ 2, z, c)


def other_core(o, z, c):
    return (o, z, 1 - c)


def paired_body(p_factor, q_factor, truncation):
    own_i, bonds, columns = p_factor.shape
    bond = q_factor.shape[0]
    half_i = own_i // 2
    half_rows = half_i * bond
    total_columns = columns * lax.axis_size("inner")
    outer = lax.axis_index("outer")
    inner = lax.axis_index("inner")
    core = inner % 2
    cut = (half_i + 1) // 2
    p4 = p_factor.reshape(2, half_i, bonds, columns)

    chunks = [contract_chunk(p4, q_factor, lo, hi) for lo, hi in ((0, cut), (cut, half_i))]
    slab = jnp.concatenate([jnp.concatenate([left, right], axis=2) for left, right in chunks], axis=1)
    slab = slab.reshape(2 * half_rows, columns)

    local_term = lax.dot_general(truncation, slab, (((0,), (0,)), ((), ())), preferred_element_type=F32)

    core_vec = core.astype(jnp.int32).reshape(1)
    outer_vec = outer.astype(jnp.int32).reshape(1)
    sums = []
    for left, right in chunks:
        x0 = move(left, to_x, low_rule)
        y1 = move(right, to_y, high_rule)
        x1 = move(right, to_x, low_rule)
        y0 = move(left, to_y, high_rule)
        d0 = move(x0, to_y, low_rule)
        d1 = move(y1, to_x, high_rule)
        keep, send = gram_chunk(core_vec, (left, right, x0, x1, y0, y1, d0, d1), slab)
        merged = merge_chunk(outer_vec, keep, move(send, other_core))
        got = lax.all_to_all(
            merged, "inner", 0, 0, axis_index_groups=[[0, 2, 4, 6], [1, 3, 5, 7]], tiled=True
        )
        sums.append(jnp.sum(got.astype(F32), axis=0))
    value = jnp.concatenate(sums, axis=0) / total_columns

    first, second = value[:, :half_rows], value[:, half_rows:]
    same = jnp.where(core == 0, first, second).astype(BF16).T
    cross = jnp.where(core == 0, second, first).astype(BF16).T
    same = move(same, lambda o, z, c: (z, o, c), off_diagonal).astype(F32)
    cross = move(cross, lambda o, z, c: (z, o, 1 - c), off_diagonal).astype(F32)
    mirror = jnp.concatenate(
        [jnp.where(core == 0, same, cross), jnp.where(core == 0, cross, same)], axis=1
    )
    gram = (value + mirror).T

    absorbed = local_term + move(local_term, to_x)
    absorbed = absorbed + move(absorbed, to_y)
    squares = lax.psum(jnp.sum(absorbed * absorbed), "inner")
    norm_scale = jnp.sqrt(squares / (absorbed.shape[0] * total_columns) + 1e-06)
    return (gram, absorbed / norm_scale)


def general_body(p_factor, q_factor, truncation):
    own_i, bonds, columns = p_factor.shape
    bond = q_factor.shape[0]
    paired = jnp.einsum("imc,jmc->ijc", p_factor, q_factor, preferred_element_type=F32)
    paired = paired / math.sqrt(bonds)
    own_rows = paired.reshape(own_i * bond, columns).astype(BF16)
    gathered = lax.all_gather(own_rows, "outer", axis=0, tiled=True)
    partial = lax.dot_general(own_rows, gathered, (((1,), (1,)), ((), ())), preferred_element_type=F32)
    total_columns = columns * lax.axis_size("inner")
    gram = lax.psum_scatter(partial, "inner", scatter_dimension=1, tiled=True) / total_columns
    local_term = lax.dot_general(truncation, own_rows, (((0,), (0,)), ((), ())), preferred_element_type=F32)
    absorbed = lax.psum(local_term, "outer")
    squares = lax.psum(jnp.sum(absorbed * absorbed), "inner")
    norm_scale = jnp.sqrt(squares / (absorbed.shape[0] * total_columns) + 1e-06)
    return (gram, absorbed / norm_scale)


def solution(mesh):
    paired = mesh.shape["outer"] == 4 and mesh.shape["inner"] == 8
    return jax.shard_map(
        paired_body if paired else general_body,
        mesh=mesh,
        in_specs=(P("outer", None, "inner"), P(None, None, "inner"), P("outer", None)),
        out_specs=(P("outer", "inner"), P(None, "inner")),
        check_vma=False,
    )
```

```python
import functools
import math

import jax
import jax.numpy as jnp
from jax import lax
from jax.experimental import pallas as pl
from jax.experimental.pallas import tpu as pltpu
from jax.sharding import PartitionSpec as P

F32 = jnp.float32
BF16 = jnp.bfloat16
AXES = ("outer", "inner")
COLUMN_TILE = 256
CUTS = (0, 2, 5, 7)


def product_rows(p_ref, q_ref, rows, cols, scale, store):
    bond = q_ref.shape[0]

    def step(group, carry):
        base = pl.multiple_of(group * 8, 8)
        q_rows = [q_ref[base + u, :, cols].astype(F32) for u in range(8)]
        for half, i in rows:
            p_row = p_ref[half, i, :, cols].astype(F32)
            sums = [jnp.sum(p_row * q_row, axis=0, keepdims=True) for q_row in q_rows]
            store(half, i, base, (jnp.concatenate(sums, axis=0) * scale).astype(BF16))
        return carry

    lax.fori_loop(0, bond // 8, step, 0)


def head_kernel(hi, scale, p_ref, q_ref, out_ref):
    bond = q_ref.shape[0]
    rows = [(h, i) for h in range(2) for i in range(hi)]
    for c in range(0, p_ref.shape[3], 128):
        cols = slice(c, c + 128)

        def store(half, i, base, value):
            out_ref[half, pl.ds(i * bond + base, 8), cols] = value

        product_rows(p_ref, q_ref, rows, cols, scale, store)


def tail_kernel(cuts, scale, p_ref, q_ref, head_ref, slab_ref, *out_refs):
    bond = q_ref.shape[0]
    rows = [(h, i) for h in range(2) for i in range(cuts[0], cuts[-1])]
    slab_ref[:, : cuts[0] * bond, :] = head_ref[...]
    for c in range(0, p_ref.shape[3], 128):
        cols = slice(c, c + 128)

        def store(half, i, base, value):
            slab_ref[half, pl.ds(i * bond + base, 8), cols] = value
            for part, out_ref in enumerate(out_refs):
                if cuts[part] <= i < cuts[part + 1]:
                    out_ref[half, pl.ds((i - cuts[part]) * bond + base, 8), cols] = value

        product_rows(p_ref, q_ref, rows, cols, scale, store)


def factor_specs(p4, q_factor):
    tile = COLUMN_TILE
    _, half_i, bonds, _ = p4.shape
    return [
        pl.BlockSpec((2, half_i, bonds, tile), lambda c: (0, 0, 0, c)),
        pl.BlockSpec((q_factor.shape[0], bonds, tile), lambda c: (0, 0, c)),
    ]


def row_spec(rows):
    return pl.BlockSpec((2, rows, COLUMN_TILE), lambda c: (0, 0, c))


def product_cost(p4, q_factor, share):
    flops = 1400 * share * p4.size * q_factor.shape[0]
    return pl.CostEstimate(flops=int(flops), bytes_accessed=2 * (p4.size + q_factor.size), transcendentals=0)


def contract(p4, q_factor, cuts):
    _, half_i, bonds, columns = p4.shape
    bond = q_factor.shape[0]
    scale = 1.0 / math.sqrt(bonds)
    params = pltpu.CompilerParams(vmem_limit_bytes=52 << 20)
    head_rows = cuts[1] * bond
    head = pl.pallas_call(
        functools.partial(head_kernel, cuts[1], scale),
        grid=(columns // COLUMN_TILE,),
        in_specs=factor_specs(p4, q_factor),
        out_specs=row_spec(head_rows),
        out_shape=jax.ShapeDtypeStruct((2, head_rows, columns), BF16),
        compiler_params=params,
        cost_estimate=product_cost(p4, q_factor, cuts[1] / half_i),
        name="contract_head",
    )(p4, q_factor)
    sizes = [half_i * bond] + [(b - a) * bond for a, b in zip(cuts[1:-1], cuts[2:])]
    slab, *rest = pl.pallas_call(
        functools.partial(tail_kernel, cuts[1:], scale),
        grid=(columns // COLUMN_TILE,),
        in_specs=factor_specs(p4, q_factor) + [row_spec(head_rows)],
        out_specs=[row_spec(s) for s in sizes],
        out_shape=[jax.ShapeDtypeStruct((2, s, columns), BF16) for s in sizes],
        compiler_params=params,
        cost_estimate=product_cost(p4, q_factor, 1 - cuts[1] / half_i),
        name="contract_tail",
    )(p4, q_factor, head)
    return slab, [head, *rest]


def gram_kernel(row0, core_ref, x_ref, y_ref, d_ref, s_ref, t_ref, *refs):
    keep_ref, send_ref, sum_ref = refs[-3:]
    core = core_ref[0]
    rows = x_ref.shape[1]
    half_rows = s_ref.shape[0] // 2
    total = jnp.zeros(sum_ref.shape, F32) if len(refs) == 3 else refs[0][...]
    for k, block in enumerate((None, x_ref, y_ref, d_ref)):
        for h in range(2):
            if block is None:
                left = s_ref[h * half_rows + row0 : h * half_rows + row0 + rows, :]
            else:
                left = block[h]
            value = lax.dot_general(
                left, s_ref[...], (((1,), (1,)), ((), ())), preferred_element_type=F32
            ).astype(BF16)
            total = total + jnp.dot(t_ref[k, h], left, preferred_element_type=F32)

            @pl.when(core == h)
            def _():
                keep_ref[k] = value

            @pl.when(core != h)
            def _():
                send_ref[k] = value

    sum_ref[...] = total


def gram_chunk(core, row0, blocks, slab, maps, running):
    rows = blocks[0].shape[1]
    total, columns = slab.shape
    out = jax.ShapeDtypeStruct((4, rows, total), BF16)
    vmem = pl.BlockSpec(memory_space=pltpu.VMEM)
    args = (*blocks, slab, maps) + (() if running is None else (running,))
    return pl.pallas_call(
        functools.partial(gram_kernel, row0),
        in_specs=[pl.BlockSpec(memory_space=pltpu.SMEM)] + [vmem] * len(args),
        out_specs=[vmem] * 3,
        out_shape=[out, out, jax.ShapeDtypeStruct((maps.shape[2], columns), F32)],
        compiler_params=pltpu.CompilerParams(vmem_limit_bytes=40 << 20),
        cost_estimate=pl.CostEstimate(
            flops=2 * 8 * 2 * rows * total * columns, bytes_accessed=12 << 20, transcendentals=0
        ),
        name="gram",
    )(core, *args)


def merge_kernel(o_ref, keep_ref, recv_ref, out_ref):
    out_ref[...] = (keep_ref[...].astype(F32) + recv_ref[...].astype(F32)).astype(BF16)


def merge_chunk(outer_index, keep, recv):
    _, rows, total = keep.shape
    spec = pl.BlockSpec((1, rows, total), lambda d, o: (d ^ o[0], 0, 0))
    return pl.pallas_call(
        merge_kernel,
        grid_spec=pltpu.PrefetchScalarGridSpec(
            num_scalar_prefetch=1,
            grid=(4,),
            in_specs=[spec, spec],
            out_specs=pl.BlockSpec((1, rows, total), lambda d, o: (d, 0, 0)),
        ),
        out_shape=jax.ShapeDtypeStruct(keep.shape, BF16),
        name="merge",
    )(outer_index, keep, recv)


def pairs(target):
    found = []
    for o in range(4):
        for z in range(4):
            for c in range(2):
                t = target(o, z, c)
                found.append((o * 8 + z * 2 + c, t[0] * 8 + t[1] * 2 + t[2]))
    return found


def move(value, target):
    return lax.ppermute(value, AXES, pairs(target))


def to_x(o, z, c):
    return (o ^ 1, z, c)


def to_y(o, z, c):
    return (o ^ 2, z, c)


def other_core(o, z, c):
    return (o, z, 1 - c)


def paired_body(p_factor, q_factor, truncation):
    own_i, bonds, columns = p_factor.shape
    bond = q_factor.shape[0]
    half_i = own_i // 2
    half_rows = half_i * bond
    total_columns = columns * lax.axis_size("inner")
    outer = lax.axis_index("outer")
    core = lax.axis_index("inner") % 2
    core_vec = core.astype(jnp.int32).reshape(1)
    outer_vec = outer.astype(jnp.int32).reshape(1)
    p4 = p_factor.reshape(2, half_i, bonds, columns)

    maps = lax.all_gather(truncation, "outer", axis=0, tiled=False)
    maps = jnp.stack([maps[outer ^ k] for k in range(4)])
    maps = maps.reshape(4, 2, half_rows, truncation.shape[1]).swapaxes(2, 3)

    slab, chunks = contract(p4, q_factor, CUTS)
    slab = slab.reshape(2 * half_rows, columns)

    sums = []
    absorbed = None
    for t, own in enumerate(chunks):
        row0, row1 = CUTS[t] * bond, CUTS[t + 1] * bond
        x = move(own, to_x)
        y = move(own, to_y)
        d = move(x, to_y) if t % 2 == 0 else move(y, to_x)
        keep, send, absorbed = gram_chunk(
            core_vec, row0, (x, y, d), slab, maps[:, :, :, row0:row1], absorbed
        )
        merged = merge_chunk(outer_vec, keep, move(send, other_core))
        got = lax.all_to_all(
            merged, "inner", 0, 0, axis_index_groups=[[0, 2, 4, 6], [1, 3, 5, 7]], tiled=True
        )
        sums.append(jnp.sum(got.astype(F32), axis=0))
    gram = (jnp.concatenate(sums, axis=0) / total_columns).T

    squares = lax.psum(jnp.sum(absorbed * absorbed), "inner")
    norm_scale = jnp.sqrt(squares / (absorbed.shape[0] * total_columns) + 1e-06)
    return (gram, absorbed / norm_scale)


def general_body(p_factor, q_factor, truncation):
    own_i, bonds, columns = p_factor.shape
    bond = q_factor.shape[0]
    paired = jnp.einsum("imc,jmc->ijc", p_factor, q_factor, preferred_element_type=F32)
    paired = paired / math.sqrt(bonds)
    own_rows = paired.reshape(own_i * bond, columns).astype(BF16)
    gathered = lax.all_gather(own_rows, "outer", axis=0, tiled=True)
    partial = lax.dot_general(own_rows, gathered, (((1,), (1,)), ((), ())), preferred_element_type=F32)
    total_columns = columns * lax.axis_size("inner")
    gram = lax.psum_scatter(partial, "inner", scatter_dimension=1, tiled=True) / total_columns
    local_term = lax.dot_general(truncation, own_rows, (((0,), (0,)), ((), ())), preferred_element_type=F32)
    absorbed = lax.psum(local_term, "outer")
    squares = lax.psum(jnp.sum(absorbed * absorbed), "inner")
    norm_scale = jnp.sqrt(squares / (absorbed.shape[0] * total_columns) + 1e-06)
    return (gram, absorbed / norm_scale)


def solution(mesh):
    paired = mesh.shape["outer"] == 4 and mesh.shape["inner"] == 8
    return jax.shard_map(
        paired_body if paired else general_body,
        mesh=mesh,
        in_specs=(P("outer", None, "inner"), P(None, None, "inner"), P("outer", None)),
        out_specs=(P("outer", "inner"), P(None, "inner")),
        check_vma=False,
    )
```

```python
import functools
import math

import jax
import jax.numpy as jnp
from jax import lax
from jax.experimental import pallas as pl
from jax.experimental.pallas import tpu as pltpu
from jax.sharding import PartitionSpec as P

F32 = jnp.float32
BF16 = jnp.bfloat16
AXES = ("outer", "inner")
COLUMN_TILE = 256
CUTS = (0, 2, 5, 7)


def product_rows(p_ref, q_ref, rows, cols, scale, store):
    bond = q_ref.shape[0]

    def step(group, carry):
        base = pl.multiple_of(group * 8, 8)
        q_rows = [q_ref[base + u, :, cols].astype(F32) for u in range(8)]
        for half, i in rows:
            p_row = p_ref[half, i, :, cols].astype(F32)
            sums = [jnp.sum(p_row * q_row, axis=0, keepdims=True) for q_row in q_rows]
            store(half, i, base, (jnp.concatenate(sums, axis=0) * scale).astype(BF16))
        return carry

    lax.fori_loop(0, bond // 8, step, 0)


def chunk_kernel(lo, hi, scale, p_ref, q_ref, out_ref):
    bond = q_ref.shape[0]
    rows = [(h, i) for h in range(2) for i in range(lo, hi)]
    for c in range(0, p_ref.shape[3], 128):
        cols = slice(c, c + 128)

        def store(half, i, base, value):
            out_ref[half, pl.ds((i - lo) * bond + base, 8), cols] = value

        product_rows(p_ref, q_ref, rows, cols, scale, store)


def last_kernel(cuts, scale, p_ref, q_ref, *refs):
    bond = q_ref.shape[0]
    earlier, (out_ref, slab_ref) = refs[:-2], refs[-2:]
    lo, hi = cuts[-2:]
    rows = [(h, i) for h in range(2) for i in range(lo, hi)]
    for part, ref in enumerate(earlier):
        slab_ref[:, cuts[part] * bond : cuts[part + 1] * bond, :] = ref[...]
    for c in range(0, p_ref.shape[3], 128):
        cols = slice(c, c + 128)

        def store(half, i, base, value):
            out_ref[half, pl.ds((i - lo) * bond + base, 8), cols] = value
            slab_ref[half, pl.ds(i * bond + base, 8), cols] = value

        product_rows(p_ref, q_ref, rows, cols, scale, store)


def contract(p4, q_factor, cuts):
    _, half_i, bonds, columns = p4.shape
    bond = q_factor.shape[0]
    scale = 1.0 / math.sqrt(bonds)
    tile = COLUMN_TILE

    def row_spec(rows):
        return pl.BlockSpec((2, rows, tile), lambda c: (0, 0, c))

    def row_shape(rows):
        return jax.ShapeDtypeStruct((2, rows, columns), BF16)

    factor_specs = [
        pl.BlockSpec((2, half_i, bonds, tile), lambda c: (0, 0, 0, c)),
        pl.BlockSpec((bond, bonds, tile), lambda c: (0, 0, c)),
    ]
    chunks = []
    for lo, hi in zip(cuts, cuts[1:]):
        last = hi == cuts[-1]
        rows = (hi - lo) * bond
        flops = 1400 * 2 * (hi - lo) * bonds * columns * bond
        earlier = chunks if last else []
        found = pl.pallas_call(
            functools.partial(last_kernel, cuts, scale) if last else functools.partial(chunk_kernel, lo, hi, scale),
            grid=(columns // tile,),
            in_specs=factor_specs + [row_spec(e.shape[1]) for e in earlier],
            out_specs=[row_spec(rows)] + ([row_spec(half_i * bond)] if last else []),
            out_shape=[row_shape(rows)] + ([row_shape(half_i * bond)] if last else []),
            compiler_params=pltpu.CompilerParams(vmem_limit_bytes=52 << 20),
            cost_estimate=pl.CostEstimate(flops=30_000_000_000, bytes_accessed=1000, transcendentals=0),
            name="contract",
        )(p4, q_factor, *earlier)
        own = found[0]
        if not last:
            q_factor, own = lax.optimization_barrier((q_factor, own))
        chunks.append(own)
    return found[1], chunks


def gram_kernel(core_ref, own_ref, x_ref, y_ref, d_ref, s_ref, t_ref, *refs):
    keep_ref, send_ref, sum_ref = refs[-3:]
    core = core_ref[0]
    rows = x_ref.shape[1]
    terms = []
    for k, block in enumerate((own_ref, x_ref, y_ref, d_ref)):
        left = block[...].reshape(2 * rows, block.shape[2])
        value = lax.dot_general(
            left, s_ref[...], (((1,), (1,)), ((), ())), preferred_element_type=F32
        ).astype(BF16)
        terms.append(jnp.dot(t_ref[k], left, preferred_element_type=F32))

        @pl.when(core == 0)
        def _():
            keep_ref[k] = value[:rows]
            send_ref[k] = value[rows:]

        @pl.when(core != 0)
        def _():
            keep_ref[k] = value[rows:]
            send_ref[k] = value[:rows]

    total = (terms[0] + terms[1]) + (terms[2] + terms[3])
    sum_ref[...] = total if len(refs) == 3 else refs[0][...] + total


def gram_chunk(core, blocks, slab, maps, running):
    rows = blocks[0].shape[1]
    total, columns = slab.shape
    out = jax.ShapeDtypeStruct((4, rows, total), BF16)
    vmem = pl.BlockSpec(memory_space=pltpu.VMEM)
    args = (*blocks, slab, maps) + (() if running is None else (running,))
    return pl.pallas_call(
        gram_kernel,
        in_specs=[pl.BlockSpec(memory_space=pltpu.SMEM)] + [vmem] * len(args),
        out_specs=[vmem] * 3,
        out_shape=[out, out, jax.ShapeDtypeStruct((maps.shape[1], columns), F32)],
        compiler_params=pltpu.CompilerParams(vmem_limit_bytes=40 << 20),
        cost_estimate=pl.CostEstimate(
            flops=1000, bytes_accessed=1000, transcendentals=0
        ),
        name="gram",
    )(core, *args)


def merge_kernel(o_ref, keep_ref, recv_ref, out_ref):
    o = o_ref[0]
    for d in range(4):
        k = d ^ o
        out_ref[d] = (keep_ref[k].astype(F32) + recv_ref[k].astype(F32)).astype(BF16)


def merge_chunk(outer_index, keep, recv):
    vmem = pl.BlockSpec(memory_space=pltpu.VMEM)
    return pl.pallas_call(
        merge_kernel,
        in_specs=[pl.BlockSpec(memory_space=pltpu.SMEM), vmem, vmem],
        out_specs=vmem,
        out_shape=jax.ShapeDtypeStruct(keep.shape, BF16),
        cost_estimate=pl.CostEstimate(flops=1000, bytes_accessed=1000, transcendentals=0),
        name="merge",
    )(outer_index, keep, recv)


def pairs(target):
    found = []
    for o in range(4):
        for z in range(4):
            for c in range(2):
                t = target(o, z, c)
                found.append((o * 8 + z * 2 + c, t[0] * 8 + t[1] * 2 + t[2]))
    return found


def move(value, target):
    return lax.ppermute(value, AXES, pairs(target))


def to_x(o, z, c):
    return (o ^ 1, z, c)


def to_y(o, z, c):
    return (o ^ 2, z, c)


def to_diagonal(o, z, c):
    return (o ^ 3, z, c)


def to_z1(o, z, c):
    return (o, z ^ 1, c)


def to_z2(o, z, c):
    return (o, z ^ 2, c)


def other_core(o, z, c):
    return (o, z, 1 - c)


def paired_body(p_factor, q_factor, truncation):
    own_i, bonds, columns = p_factor.shape
    bond = q_factor.shape[0]
    half_i = own_i // 2
    half_rows = half_i * bond
    total_columns = columns * lax.axis_size("inner")
    outer = lax.axis_index("outer")
    core = lax.axis_index("inner") % 2
    core_vec = core.astype(jnp.int32).reshape(1)
    outer_vec = outer.astype(jnp.int32).reshape(1)
    p4 = p_factor.reshape(2, half_i, bonds, columns)

    maps = [truncation] + [move(truncation, to) for to in (to_x, to_y, to_diagonal)]
    maps = jnp.stack(maps).reshape(4, 2, half_rows, truncation.shape[1])
    slab, chunks = contract(p4, q_factor, CUTS)
    slab = slab.reshape(2 * half_rows, columns)

    moved = []
    for t, own in enumerate(chunks):
        x = move(own, to_x)
        y = move(own, to_y)
        d = move(x, to_y) if t % 2 == 0 else move(y, to_x)
        moved.append([x, y, d])

    sums = []
    absorbed = None
    merged = None
    for t, own in enumerate(chunks):
        row0, row1 = CUTS[t] * bond, CUTS[t + 1] * bond
        if merged is not None:
            moved[t][2], merged = lax.optimization_barrier((moved[t][2], merged))
            sums.append(merged)
        if t + 1 < len(chunks):
            moved[t][2], moved[t + 1][0], moved[t + 1][1] = lax.optimization_barrier(
                (moved[t][2], moved[t + 1][0], moved[t + 1][1])
            )
        part = maps[:, :, row0:row1].reshape(4, 2 * (row1 - row0), -1).swapaxes(1, 2)
        keep, send, absorbed = gram_chunk(core_vec, (own, *moved[t]), slab, part, absorbed)
        merged = merge_chunk(outer_vec, keep, move(send, other_core))
    sums.append(merged)
    sums = [
        lax.all_to_all(m, "inner", 0, 0, axis_index_groups=[[0, 2, 4, 6], [1, 3, 5, 7]], tiled=True)
        for m in sums
    ]
    sums = [jnp.sum(m.astype(F32), axis=0) for m in sums]
    gram = (jnp.concatenate(sums, axis=0) / total_columns).T

    squares = jnp.full((8, 128), jnp.sum(absorbed * absorbed))
    for to in (other_core, to_z1, to_z2):
        squares = squares + move(squares, to)
    norm_scale = jnp.sqrt(squares[:1, :1] / (absorbed.shape[0] * total_columns) + 1e-06)
    return (gram, absorbed / norm_scale)


def general_body(p_factor, q_factor, truncation):
    own_i, bonds, columns = p_factor.shape
    bond = q_factor.shape[0]
    paired = jnp.einsum("imc,jmc->ijc", p_factor, q_factor, preferred_element_type=F32)
    paired = paired / math.sqrt(bonds)
    own_rows = paired.reshape(own_i * bond, columns).astype(BF16)
    gathered = lax.all_gather(own_rows, "outer", axis=0, tiled=True)
    partial = lax.dot_general(own_rows, gathered, (((1,), (1,)), ((), ())), preferred_element_type=F32)
    total_columns = columns * lax.axis_size("inner")
    gram = lax.psum_scatter(partial, "inner", scatter_dimension=1, tiled=True) / total_columns
    local_term = lax.dot_general(truncation, own_rows, (((0,), (0,)), ((), ())), preferred_element_type=F32)
    absorbed = lax.psum(local_term, "outer")
    squares = lax.psum(jnp.sum(absorbed * absorbed), "inner")
    norm_scale = jnp.sqrt(squares / (absorbed.shape[0] * total_columns) + 1e-06)
    return (gram, absorbed / norm_scale)


def solution(mesh):
    paired = mesh.shape["outer"] == 4 and mesh.shape["inner"] == 8
    return jax.shard_map(
        paired_body if paired else general_body,
        mesh=mesh,
        in_specs=(P("outer", None, "inner"), P(None, None, "inner"), P("outer", None)),
        out_specs=(P("outer", "inner"), P(None, "inner")),
        check_vma=False,
    )
```

```python
import functools
import math

import jax
import jax.numpy as jnp
from jax import lax
from jax.experimental import pallas as pl
from jax.experimental.pallas import tpu as pltpu
from jax.sharding import PartitionSpec as P

F32 = jnp.float32
BF16 = jnp.bfloat16
AXES = ("outer", "inner")
COLUMN_TILE = 256
CUTS = (0, 2, 5, 7)
ROUTES = "yxy"
XY_DUE = ()
Z_DUE = ()
Z_SEND = (1, 2)
XY_SEND = (0,)
D_SEND = (1,)
GATE = True
GRAM_VMEM = 20
GRAM_FLOPS = 4_000_000_000
MERGE_VMEM = 8
CONTRACT_FLOPS = 30_000_000_000


def product_rows(p_ref, q_ref, rows, cols, scale, store):
    bond = q_ref.shape[0]

    def step(group, carry):
        base = pl.multiple_of(group * 8, 8)
        q_rows = [q_ref[base + u, :, cols].astype(F32) for u in range(8)]
        for half, i in rows:
            p_row = p_ref[half, i, :, cols].astype(F32)
            sums = [jnp.sum(p_row * q_row, axis=0, keepdims=True) for q_row in q_rows]
            store(half, i, base, (jnp.concatenate(sums, axis=0) * scale).astype(BF16))
        return carry

    lax.fori_loop(0, bond // 8, step, 0)


def chunk_kernel(lo, hi, scale, p_ref, q_ref, out_ref):
    bond = q_ref.shape[0]
    rows = [(h, i) for h in range(2) for i in range(lo, hi)]
    for c in range(0, p_ref.shape[3], 128):
        cols = slice(c, c + 128)

        def store(half, i, base, value):
            out_ref[half, pl.ds((i - lo) * bond + base, 8), cols] = value

        product_rows(p_ref, q_ref, rows, cols, scale, store)


def last_kernel(cuts, scale, p_ref, q_ref, *refs):
    bond = q_ref.shape[0]
    earlier, (out_ref, slab_ref) = refs[:-2], refs[-2:]
    lo, hi = cuts[-2:]
    rows = [(h, i) for h in range(2) for i in range(lo, hi)]
    for part, ref in enumerate(earlier):
        slab_ref[:, cuts[part] * bond : cuts[part + 1] * bond, :] = ref[...]
    for c in range(0, p_ref.shape[3], 128):
        cols = slice(c, c + 128)

        def store(half, i, base, value):
            out_ref[half, pl.ds((i - lo) * bond + base, 8), cols] = value
            slab_ref[half, pl.ds(i * bond + base, 8), cols] = value

        product_rows(p_ref, q_ref, rows, cols, scale, store)


def contract(p4, q_factor, cuts, maps):
    _, half_i, bonds, columns = p4.shape
    bond = q_factor.shape[0]
    scale = 1.0 / math.sqrt(bonds)
    tile = COLUMN_TILE

    def row_spec(rows):
        return pl.BlockSpec((2, rows, tile), lambda c: (0, 0, c))

    def row_shape(rows):
        return jax.ShapeDtypeStruct((2, rows, columns), BF16)

    factor_specs = [
        pl.BlockSpec((2, half_i, bonds, tile), lambda c: (0, 0, 0, c)),
        pl.BlockSpec((bond, bonds, tile), lambda c: (0, 0, c)),
    ]
    chunks = []
    for lo, hi in zip(cuts, cuts[1:]):
        last = hi == cuts[-1]
        rows = (hi - lo) * bond
        flops = 1400 * 2 * (hi - lo) * bonds * columns * bond
        earlier = chunks if last else []
        found = pl.pallas_call(
            functools.partial(last_kernel, cuts, scale) if last else functools.partial(chunk_kernel, lo, hi, scale),
            grid=(columns // tile,),
            in_specs=factor_specs + [row_spec(e.shape[1]) for e in earlier],
            out_specs=[row_spec(rows)] + ([row_spec(half_i * bond)] if last else []),
            out_shape=[row_shape(rows)] + ([row_shape(half_i * bond)] if last else []),
            compiler_params=pltpu.CompilerParams(vmem_limit_bytes=52 << 20),
            cost_estimate=pl.CostEstimate(flops=CONTRACT_FLOPS, bytes_accessed=1000, transcendentals=0),
            name="contract",
        )(p4, q_factor, *earlier)
        own = found[0]
        if not last:
            q_factor, own, maps = lax.optimization_barrier((q_factor, own, maps))
        chunks.append(own)
    return found[1], chunks, maps


def gram_kernel(core_ref, own_ref, x_ref, y_ref, d_ref, s_ref, t_ref, *refs):
    keep_ref, send_ref, sum_ref = refs[-3:]
    core = core_ref[0]
    rows = x_ref.shape[1]
    terms = []
    for k, block in enumerate((own_ref, x_ref, y_ref, d_ref)):
        left = block[...].reshape(2 * rows, block.shape[2])
        value = lax.dot_general(
            left, s_ref[...], (((1,), (1,)), ((), ())), preferred_element_type=F32
        ).astype(BF16)
        terms.append(jnp.dot(t_ref[k], left, preferred_element_type=F32))

        @pl.when(core == 0)
        def _():
            keep_ref[k] = value[:rows]
            send_ref[k] = value[rows:]

        @pl.when(core != 0)
        def _():
            keep_ref[k] = value[rows:]
            send_ref[k] = value[:rows]

    total = (terms[0] + terms[1]) + (terms[2] + terms[3])
    sum_ref[...] = total if len(refs) == 3 else refs[0][...] + total


def gram_chunk(core, blocks, slab, maps, running):
    rows = blocks[0].shape[1]
    total, columns = slab.shape
    out = jax.ShapeDtypeStruct((4, rows, total), BF16)
    vmem = pl.BlockSpec(memory_space=pltpu.VMEM)
    args = (*blocks, slab, maps) + (() if running is None else (running,))
    return pl.pallas_call(
        gram_kernel,
        in_specs=[pl.BlockSpec(memory_space=pltpu.SMEM)] + [vmem] * len(args),
        out_specs=[vmem] * 3,
        out_shape=[out, out, jax.ShapeDtypeStruct((maps.shape[1], columns), F32)],
        compiler_params=pltpu.CompilerParams(vmem_limit_bytes=GRAM_VMEM << 20),
        cost_estimate=pl.CostEstimate(
            flops=GRAM_FLOPS, bytes_accessed=1000, transcendentals=0
        ),
        name="gram",
    )(core, *args)


def merge_kernel(place_ref, keep_ref, recv_ref, *out_refs):
    for shift, out_ref in enumerate(out_refs):
        k = place_ref[0] ^ place_ref[1] ^ shift
        out_ref[...] = (keep_ref[k].astype(F32) + recv_ref[k].astype(F32)).astype(BF16)


def merge_chunk(place, keep, recv):
    vmem = pl.BlockSpec(memory_space=pltpu.VMEM)
    return pl.pallas_call(
        merge_kernel,
        in_specs=[pl.BlockSpec(memory_space=pltpu.SMEM), vmem, vmem],
        out_specs=[vmem] * 4,
        out_shape=[jax.ShapeDtypeStruct(keep.shape[1:], BF16)] * 4,
        compiler_params=pltpu.CompilerParams(vmem_limit_bytes=MERGE_VMEM << 20),
        cost_estimate=pl.CostEstimate(flops=1000, bytes_accessed=1000, transcendentals=0),
        name="merge",
    )(place, keep, recv)


def pairs(target):
    found = []
    for o in range(4):
        for z in range(4):
            for c in range(2):
                t = target(o, z, c)
                found.append((o * 8 + z * 2 + c, t[0] * 8 + t[1] * 2 + t[2]))
    return found


def move(value, target):
    return lax.ppermute(value, AXES, pairs(target))


def to_x(o, z, c):
    return (o ^ 1, z, c)


def to_y(o, z, c):
    return (o ^ 2, z, c)


def to_diagonal(o, z, c):
    return (o ^ 3, z, c)


def to_z1(o, z, c):
    return (o, z ^ 1, c)


def to_z2(o, z, c):
    return (o, z ^ 2, c)


def to_z3(o, z, c):
    return (o, z ^ 3, c)


def other_core(o, z, c):
    return (o, z, 1 - c)


def paired_body(p_factor, q_factor, truncation):
    own_i, bonds, columns = p_factor.shape
    bond = q_factor.shape[0]
    half_i = own_i // 2
    half_rows = half_i * bond
    total_columns = columns * lax.axis_size("inner")
    outer = lax.axis_index("outer")
    core = lax.axis_index("inner") % 2
    core_vec = core.astype(jnp.int32).reshape(1)
    place = jnp.stack([outer, lax.axis_index("inner") // 2]).astype(jnp.int32)
    p4 = p_factor.reshape(2, half_i, bonds, columns)

    maps = [truncation] + [move(truncation, to) for to in (to_x, to_y, to_diagonal)]
    slab, chunks, maps = contract(p4, q_factor, CUTS, maps)
    maps = jnp.stack(maps).reshape(4, 2, half_rows, truncation.shape[1])
    slab = slab.reshape(2 * half_rows, columns)

    moved = []
    for t, own in enumerate(chunks):
        x = move(own, to_x)
        y = move(own, to_y)
        x, y = lax.optimization_barrier((x, y))
        if ROUTES[t] == "y":
            d = move(x, to_y)
        elif ROUTES[t] == "x":
            d = move(y, to_x)
        else:
            d = move(own, to_diagonal)
        moved.append([x, y, d])

    sums = []
    absorbed = None
    for t, own in enumerate(chunks):
        row0, row1 = CUTS[t] * bond, CUTS[t + 1] * bond
        if t in XY_DUE:
            moved[t][2], moved[t + 1][0], moved[t + 1][1] = lax.optimization_barrier(
                (moved[t][2], moved[t + 1][0], moved[t + 1][1])
            )
        if sums:
            due = sums[-1] if t in Z_DUE else sums[-1][:1]
            moved[t][2], *due = lax.optimization_barrier((moved[t][2], *due))
            sums[-1][: len(due)] = due
        part = maps[:, :, row0:row1].reshape(4, 2 * (row1 - row0), -1).swapaxes(1, 2)
        keep, send, absorbed = gram_chunk(core_vec, (own, *moved[t]), slab, part, absorbed)
        if t in Z_SEND:
            send, *sums[-1] = lax.optimization_barrier((send, *sums[-1]))
        if t in XY_SEND:
            send, moved[t + 1][0], moved[t + 1][1] = lax.optimization_barrier(
                (send, moved[t + 1][0], moved[t + 1][1])
            )
        if t in D_SEND:
            send, moved[t + 1][2] = lax.optimization_barrier((send, moved[t + 1][2]))
        recv = move(send, other_core)
        pieces = merge_chunk(place, keep, recv)
        pieces = list(pieces)
        sums.append(pieces[:1] + [move(v, to) for v, to in zip(pieces[1:], (to_z1, to_z2, to_z3))])
    group = sums[-1]

    squares = jnp.full((8, 128), jnp.sum(absorbed * absorbed))
    squares = squares + move(squares, other_core)
    if GATE:
        squares, group[1] = lax.optimization_barrier((squares, group[1]))
    across = [move(squares, to) for to in (to_z1, to_z2, to_z3)]
    squares = (squares + across[0]) + (across[1] + across[2])
    sums = [sum(v.astype(F32) for v in group) for group in sums]
    gram = (jnp.concatenate(sums, axis=0) / total_columns).T
    norm_scale = jnp.sqrt(squares[:1, :1] / (absorbed.shape[0] * total_columns) + 1e-06)
    return (gram, absorbed / norm_scale)


def general_body(p_factor, q_factor, truncation):
    own_i, bonds, columns = p_factor.shape
    bond = q_factor.shape[0]
    paired = jnp.einsum("imc,jmc->ijc", p_factor, q_factor, preferred_element_type=F32)
    paired = paired / math.sqrt(bonds)
    own_rows = paired.reshape(own_i * bond, columns).astype(BF16)
    gathered = lax.all_gather(own_rows, "outer", axis=0, tiled=True)
    partial = lax.dot_general(own_rows, gathered, (((1,), (1,)), ((), ())), preferred_element_type=F32)
    total_columns = columns * lax.axis_size("inner")
    gram = lax.psum_scatter(partial, "inner", scatter_dimension=1, tiled=True) / total_columns
    local_term = lax.dot_general(truncation, own_rows, (((0,), (0,)), ((), ())), preferred_element_type=F32)
    absorbed = lax.psum(local_term, "outer")
    squares = lax.psum(jnp.sum(absorbed * absorbed), "inner")
    norm_scale = jnp.sqrt(squares / (absorbed.shape[0] * total_columns) + 1e-06)
    return (gram, absorbed / norm_scale)


def solution(mesh):
    paired = mesh.shape["outer"] == 4 and mesh.shape["inner"] == 8
    return jax.shard_map(
        paired_body if paired else general_body,
        mesh=mesh,
        in_specs=(P("outer", None, "inner"), P(None, None, "inner"), P("outer", None)),
        out_specs=(P("outer", "inner"), P(None, "inner")),
        check_vma=False,
    )
```

```python
import functools
import math

import jax
import jax.numpy as jnp
from jax import lax
from jax.experimental import pallas as pl
from jax.experimental.pallas import tpu as pltpu
from jax.sharding import PartitionSpec as P

F32 = jnp.float32
BF16 = jnp.bfloat16
AXES = ("outer", "inner")
COLUMN_TILE = 256
CUTS = (0, 2, 5, 7)
ROUTES = "yxy"
XY_DUE = ()
Z_DUE = ()
Z_PARTS = {1: (1, 2, 3), 2: (1, 2)}
XY_SEND = ()
D_SEND = (1,)
GATE = True
MAPS_AT = 1
LAST_VMEM = 52
TIE = False
X_AFTER = ()
PAIRED = (0, 1, 2)
DUE_GRAM = {}
DUE_SEND = {}
GRAM_VMEM = 20
GRAM_FLOPS = 4_000_000_000
MERGE_VMEM = 8
CONTRACT_FLOPS = 30_000_000_000


def product_rows(p_ref, q_ref, rows, cols, scale, store):
    bond = q_ref.shape[0]

    def step(group, carry):
        base = pl.multiple_of(group * 8, 8)
        q_rows = [q_ref[base + u, :, cols].astype(F32) for u in range(8)]
        for half, i in rows:
            p_row = p_ref[half, i, :, cols].astype(F32)
            sums = [jnp.sum(p_row * q_row, axis=0, keepdims=True) for q_row in q_rows]
            store(half, i, base, (jnp.concatenate(sums, axis=0) * scale).astype(BF16))
        return carry

    lax.fori_loop(0, bond // 8, step, 0)


def chunk_kernel(lo, hi, scale, p_ref, q_ref, out_ref):
    bond = q_ref.shape[0]
    rows = [(h, i) for h in range(2) for i in range(lo, hi)]
    for c in range(0, p_ref.shape[3], 128):
        cols = slice(c, c + 128)

        def store(half, i, base, value):
            out_ref[half, pl.ds((i - lo) * bond + base, 8), cols] = value

        product_rows(p_ref, q_ref, rows, cols, scale, store)


def last_kernel(cuts, scale, p_ref, q_ref, *refs):
    bond = q_ref.shape[0]
    earlier, (out_ref, slab_ref) = refs[:-2], refs[-2:]
    lo, hi = cuts[-2:]
    rows = [(h, i) for h in range(2) for i in range(lo, hi)]
    for part, ref in enumerate(earlier):
        slab_ref[:, cuts[part] * bond : cuts[part + 1] * bond, :] = ref[...]
    for c in range(0, p_ref.shape[3], 128):
        cols = slice(c, c + 128)

        def store(half, i, base, value):
            out_ref[half, pl.ds((i - lo) * bond + base, 8), cols] = value
            slab_ref[half, pl.ds(i * bond + base, 8), cols] = value

        product_rows(p_ref, q_ref, rows, cols, scale, store)


def contract(p4, q_factor, cuts, truncation):
    _, half_i, bonds, columns = p4.shape
    bond = q_factor.shape[0]
    scale = 1.0 / math.sqrt(bonds)
    tile = COLUMN_TILE

    def row_spec(rows):
        return pl.BlockSpec((2, rows, tile), lambda c: (0, 0, c))

    def row_shape(rows):
        return jax.ShapeDtypeStruct((2, rows, columns), BF16)

    factor_specs = [
        pl.BlockSpec((2, half_i, bonds, tile), lambda c: (0, 0, 0, c)),
        pl.BlockSpec((bond, bonds, tile), lambda c: (0, 0, c)),
    ]
    chunks = []
    maps = None
    if not TIE:
        maps = [truncation] + [move(truncation, to) for to in (to_x, to_y, to_diagonal)]
    for lo, hi in zip(cuts, cuts[1:]):
        last = hi == cuts[-1]
        rows = (hi - lo) * bond
        flops = 1400 * 2 * (hi - lo) * bonds * columns * bond
        earlier = chunks if last else []
        found = pl.pallas_call(
            functools.partial(last_kernel, cuts, scale) if last else functools.partial(chunk_kernel, lo, hi, scale),
            grid=(columns // tile,),
            in_specs=factor_specs + [row_spec(e.shape[1]) for e in earlier],
            out_specs=[row_spec(rows)] + ([row_spec(half_i * bond)] if last else []),
            out_shape=[row_shape(rows)] + ([row_shape(half_i * bond)] if last else []),
            compiler_params=pltpu.CompilerParams(vmem_limit_bytes=(LAST_VMEM if last else 52) << 20),
            cost_estimate=pl.CostEstimate(flops=CONTRACT_FLOPS, bytes_accessed=1000, transcendentals=0),
            name="contract",
        )(p4, q_factor, *earlier)
        own = found[0]
        if not last:
            q_factor, own = lax.optimization_barrier((q_factor, own))
            if TIE and not chunks:
                truncation, own = lax.optimization_barrier((truncation, own))
                maps = [truncation] + [move(truncation, to) for to in (to_x, to_y, to_diagonal)]
            if len(chunks) == MAPS_AT:
                q_factor, maps = lax.optimization_barrier((q_factor, maps))
        chunks.append(own)
    return found[1], chunks, maps


def gram_kernel(parts, core_ref, own_ref, x_ref, y_ref, *refs):
    diagonal, (s_ref, t_ref), refs = refs[:parts], refs[parts : parts + 2], refs[parts + 2 :]
    keep_ref, send_ref, sum_ref = refs[-3:]
    core = core_ref[0]
    rows = x_ref.shape[1]
    terms = []
    for k, block in enumerate(((own_ref,), (x_ref,), (y_ref,), diagonal)):
        left = [part[...].reshape(-1, part.shape[2]) for part in block]
        left = left[0] if len(left) == 1 else jnp.concatenate(left, axis=0)
        value = lax.dot_general(
            left, s_ref[...], (((1,), (1,)), ((), ())), preferred_element_type=F32
        ).astype(BF16)
        terms.append(jnp.dot(t_ref[k], left, preferred_element_type=F32))

        @pl.when(core == 0)
        def _():
            keep_ref[k] = value[:rows]
            send_ref[k] = value[rows:]

        @pl.when(core != 0)
        def _():
            keep_ref[k] = value[rows:]
            send_ref[k] = value[:rows]

    total = (terms[0] + terms[1]) + (terms[2] + terms[3])
    sum_ref[...] = total if len(refs) == 3 else refs[0][...] + total


def gram_chunk(core, blocks, slab, maps, running):
    rows = blocks[0].shape[1]
    total, columns = slab.shape
    out = jax.ShapeDtypeStruct((4, rows, total), BF16)
    vmem = pl.BlockSpec(memory_space=pltpu.VMEM)
    args = (*blocks, slab, maps) + (() if running is None else (running,))
    return pl.pallas_call(
        functools.partial(gram_kernel, len(blocks) - 3),
        in_specs=[pl.BlockSpec(memory_space=pltpu.SMEM)] + [vmem] * len(args),
        out_specs=[vmem] * 3,
        out_shape=[out, out, jax.ShapeDtypeStruct((maps.shape[1], columns), F32)],
        compiler_params=pltpu.CompilerParams(vmem_limit_bytes=GRAM_VMEM << 20),
        cost_estimate=pl.CostEstimate(
            flops=GRAM_FLOPS, bytes_accessed=1000, transcendentals=0
        ),
        name="gram",
    )(core, *args)


def merge_kernel(place_ref, keep_ref, recv_ref, *out_refs):
    for shift, out_ref in enumerate(out_refs):
        k = place_ref[0] ^ place_ref[1] ^ shift
        out_ref[...] = (keep_ref[k].astype(F32) + recv_ref[k].astype(F32)).astype(BF16)


def merge_chunk(place, keep, recv):
    vmem = pl.BlockSpec(memory_space=pltpu.VMEM)
    return pl.pallas_call(
        merge_kernel,
        in_specs=[pl.BlockSpec(memory_space=pltpu.SMEM), vmem, vmem],
        out_specs=[vmem] * 4,
        out_shape=[jax.ShapeDtypeStruct(keep.shape[1:], BF16)] * 4,
        compiler_params=pltpu.CompilerParams(vmem_limit_bytes=MERGE_VMEM << 20),
        cost_estimate=pl.CostEstimate(flops=1000, bytes_accessed=1000, transcendentals=0),
        name="merge",
    )(place, keep, recv)


def pairs(target):
    found = []
    for o in range(4):
        for z in range(4):
            for c in range(2):
                t = target(o, z, c)
                found.append((o * 8 + z * 2 + c, t[0] * 8 + t[1] * 2 + t[2]))
    return found


def move(value, target):
    return lax.ppermute(value, AXES, pairs(target))


def to_x(o, z, c):
    return (o ^ 1, z, c)


def to_y(o, z, c):
    return (o ^ 2, z, c)


def to_diagonal(o, z, c):
    return (o ^ 3, z, c)


def to_z1(o, z, c):
    return (o, z ^ 1, c)


def to_z2(o, z, c):
    return (o, z ^ 2, c)


def to_z3(o, z, c):
    return (o, z ^ 3, c)


def other_core(o, z, c):
    return (o, z, 1 - c)


def paired_body(p_factor, q_factor, truncation):
    own_i, bonds, columns = p_factor.shape
    bond = q_factor.shape[0]
    half_i = own_i // 2
    half_rows = half_i * bond
    total_columns = columns * lax.axis_size("inner")
    outer = lax.axis_index("outer")
    core = lax.axis_index("inner") % 2
    core_vec = core.astype(jnp.int32).reshape(1)
    place = jnp.stack([outer, lax.axis_index("inner") // 2]).astype(jnp.int32)
    p4 = p_factor.reshape(2, half_i, bonds, columns)

    slab, chunks, maps = contract(p4, q_factor, CUTS, truncation)
    maps = jnp.stack(maps).reshape(4, 2, half_rows, truncation.shape[1])
    slab = slab.reshape(2 * half_rows, columns)

    moved = []
    for t, own in enumerate(chunks):
        source = own
        if t in X_AFTER:
            source, moved[t - 1][1] = lax.optimization_barrier((own, moved[t - 1][1]))
        x = move(source, to_x)
        y = move(own, to_y)
        if t in PAIRED:
            x, y = lax.optimization_barrier((x, y))
        if ROUTES[t] == "y":
            d = move(x, to_y)
        elif ROUTES[t] == "x":
            d = move(y, to_x)
        elif ROUTES[t] == "s":
            d = (move(x[:1], to_y), move(y[1:], to_x))
        else:
            d = move(own, to_diagonal)
        moved.append([x, y, d])

    sums = []
    absorbed = None
    for t, own in enumerate(chunks):
        row0, row1 = CUTS[t] * bond, CUTS[t + 1] * bond
        for chunk, which in DUE_GRAM.get(t, ()):
            moved[t][2], moved[chunk][which] = lax.optimization_barrier((moved[t][2], moved[chunk][which]))
        if t in XY_DUE:
            moved[t][2], moved[t + 1][0], moved[t + 1][1] = lax.optimization_barrier(
                (moved[t][2], moved[t + 1][0], moved[t + 1][1])
            )
        if sums:
            due = sums[-1] if t in Z_DUE else sums[-1][:1]
            moved[t][2], *due = lax.optimization_barrier((moved[t][2], *due))
            sums[-1][: len(due)] = due
        part = maps[:, :, row0:row1].reshape(4, 2 * (row1 - row0), -1).swapaxes(1, 2)
        keep, send, absorbed = gram_chunk(core_vec, (own, *jax.tree.leaves(moved[t])), slab, part, absorbed)
        for part in Z_PARTS.get(t, ()):
            send, sums[-1][part] = lax.optimization_barrier((send, sums[-1][part]))
        for chunk, which in DUE_SEND.get(t, ()):
            send, moved[chunk][which] = lax.optimization_barrier((send, moved[chunk][which]))
        if t in XY_SEND:
            send, moved[t + 1][0], moved[t + 1][1] = lax.optimization_barrier(
                (send, moved[t + 1][0], moved[t + 1][1])
            )
        if t in D_SEND:
            send, moved[t + 1][2] = lax.optimization_barrier((send, moved[t + 1][2]))
        recv = move(send, other_core)
        pieces = merge_chunk(place, keep, recv)
        pieces = list(pieces)
        sums.append(pieces[:1] + [move(v, to) for v, to in zip(pieces[1:], (to_z1, to_z2, to_z3))])
    group = sums[-1]

    squares = jnp.full((8, 128), jnp.sum(absorbed * absorbed))
    squares = squares + move(squares, other_core)
    if GATE:
        squares, group[1] = lax.optimization_barrier((squares, group[1]))
    across = [move(squares, to) for to in (to_z1, to_z2, to_z3)]
    squares = (squares + across[0]) + (across[1] + across[2])
    sums = [sum(v.astype(F32) for v in group) for group in sums]
    gram = (jnp.concatenate(sums, axis=0) / total_columns).T
    norm_scale = jnp.sqrt(squares[:1, :1] / (absorbed.shape[0] * total_columns) + 1e-06)
    return (gram, absorbed / norm_scale)


def general_body(p_factor, q_factor, truncation):
    own_i, bonds, columns = p_factor.shape
    bond = q_factor.shape[0]
    paired = jnp.einsum("imc,jmc->ijc", p_factor, q_factor, preferred_element_type=F32)
    paired = paired / math.sqrt(bonds)
    own_rows = paired.reshape(own_i * bond, columns).astype(BF16)
    gathered = lax.all_gather(own_rows, "outer", axis=0, tiled=True)
    partial = lax.dot_general(own_rows, gathered, (((1,), (1,)), ((), ())), preferred_element_type=F32)
    total_columns = columns * lax.axis_size("inner")
    gram = lax.psum_scatter(partial, "inner", scatter_dimension=1, tiled=True) / total_columns
    local_term = lax.dot_general(truncation, own_rows, (((0,), (0,)), ((), ())), preferred_element_type=F32)
    absorbed = lax.psum(local_term, "outer")
    squares = lax.psum(jnp.sum(absorbed * absorbed), "inner")
    norm_scale = jnp.sqrt(squares / (absorbed.shape[0] * total_columns) + 1e-06)
    return (gram, absorbed / norm_scale)


def solution(mesh):
    paired = mesh.shape["outer"] == 4 and mesh.shape["inner"] == 8
    return jax.shard_map(
        paired_body if paired else general_body,
        mesh=mesh,
        in_specs=(P("outer", None, "inner"), P(None, None, "inner"), P("outer", None)),
        out_specs=(P("outer", "inner"), P(None, "inner")),
        check_vma=False,
    )
```

```python
import functools
import math

import jax
import jax.numpy as jnp
from jax import lax
from jax.experimental import pallas as pl
from jax.experimental.pallas import tpu as pltpu
from jax.sharding import PartitionSpec as P

F32 = jnp.float32
BF16 = jnp.bfloat16
AXES = ("outer", "inner")
COLUMN_TILE = 256
CUTS = (0, 2, 5, 7)
ROUTES = "yxy"
XY_DUE = ()
Z_DUE = ()
Z_PARTS = {1: (1, 2, 3), 2: (1, 2)}
XY_SEND = ()
D_SEND = (1,)
GATE = False
MAPS_AT = 1
LAST_VMEM = 52
TIE = False
X_AFTER = ()
PAIRED = (0, 1, 2)
DUE_GRAM = {}
DUE_SEND = {}
GRAM_VMEM = 20
GRAM_FLOPS = 4_000_000_000
MERGE_VMEM = 8
CONTRACT_FLOPS = 30_000_000_000


def product_rows(p_ref, q_ref, rows, cols, scale, store):
    bond = q_ref.shape[0]

    def step(group, carry):
        base = pl.multiple_of(group * 8, 8)
        q_rows = [q_ref[base + u, :, cols].astype(F32) for u in range(8)]
        for half, i in rows:
            p_row = p_ref[half, i, :, cols].astype(F32)
            sums = [jnp.sum(p_row * q_row, axis=0, keepdims=True) for q_row in q_rows]
            store(half, i, base, (jnp.concatenate(sums, axis=0) * scale).astype(BF16))
        return carry

    lax.fori_loop(0, bond // 8, step, 0)


def chunk_kernel(lo, hi, scale, p_ref, q_ref, out_ref):
    bond = q_ref.shape[0]
    rows = [(h, i) for h in range(2) for i in range(lo, hi)]
    for c in range(0, p_ref.shape[3], 128):
        cols = slice(c, c + 128)

        def store(half, i, base, value):
            out_ref[half, pl.ds((i - lo) * bond + base, 8), cols] = value

        product_rows(p_ref, q_ref, rows, cols, scale, store)


def last_kernel(cuts, scale, p_ref, q_ref, *refs):
    bond = q_ref.shape[0]
    earlier, (out_ref, slab_ref) = refs[:-2], refs[-2:]
    lo, hi = cuts[-2:]
    rows = [(h, i) for h in range(2) for i in range(lo, hi)]
    for part, ref in enumerate(earlier):
        slab_ref[:, cuts[part] * bond : cuts[part + 1] * bond, :] = ref[...]
    for c in range(0, p_ref.shape[3], 128):
        cols = slice(c, c + 128)

        def store(half, i, base, value):
            out_ref[half, pl.ds((i - lo) * bond + base, 8), cols] = value
            slab_ref[half, pl.ds(i * bond + base, 8), cols] = value

        product_rows(p_ref, q_ref, rows, cols, scale, store)


def contract(p4, q_factor, cuts, truncation):
    _, half_i, bonds, columns = p4.shape
    bond = q_factor.shape[0]
    scale = 1.0 / math.sqrt(bonds)
    tile = COLUMN_TILE

    def row_spec(rows):
        return pl.BlockSpec((2, rows, tile), lambda c: (0, 0, c))

    def row_shape(rows):
        return jax.ShapeDtypeStruct((2, rows, columns), BF16)

    factor_specs = [
        pl.BlockSpec((2, half_i, bonds, tile), lambda c: (0, 0, 0, c)),
        pl.BlockSpec((bond, bonds, tile), lambda c: (0, 0, c)),
    ]
    chunks = []
    maps = None
    if not TIE:
        maps = [truncation] + [move(truncation, to) for to in (to_x, to_y, to_diagonal)]
    for lo, hi in zip(cuts, cuts[1:]):
        last = hi == cuts[-1]
        rows = (hi - lo) * bond
        flops = 1400 * 2 * (hi - lo) * bonds * columns * bond
        earlier = chunks if last else []
        found = pl.pallas_call(
            functools.partial(last_kernel, cuts, scale) if last else functools.partial(chunk_kernel, lo, hi, scale),
            grid=(columns // tile,),
            in_specs=factor_specs + [row_spec(e.shape[1]) for e in earlier],
            out_specs=[row_spec(rows)] + ([row_spec(half_i * bond)] if last else []),
            out_shape=[row_shape(rows)] + ([row_shape(half_i * bond)] if last else []),
            compiler_params=pltpu.CompilerParams(vmem_limit_bytes=(LAST_VMEM if last else 52) << 20),
            cost_estimate=pl.CostEstimate(flops=CONTRACT_FLOPS, bytes_accessed=1000, transcendentals=0),
            name="contract",
        )(p4, q_factor, *earlier)
        own = found[0]
        if not last:
            q_factor, own = lax.optimization_barrier((q_factor, own))
            if TIE and not chunks:
                truncation, own = lax.optimization_barrier((truncation, own))
                maps = [truncation] + [move(truncation, to) for to in (to_x, to_y, to_diagonal)]
            if len(chunks) == MAPS_AT:
                q_factor, maps = lax.optimization_barrier((q_factor, maps))
        chunks.append(own)
    return found[1], chunks, maps


def gram_kernel(parts, core_ref, own_ref, x_ref, y_ref, *refs):
    diagonal, (s_ref, t_ref), refs = refs[:parts], refs[parts : parts + 2], refs[parts + 2 :]
    keep_ref, send_ref, sum_ref = refs[-3:]
    core = core_ref[0]
    rows = x_ref.shape[1]
    terms = []
    for k, block in enumerate(((own_ref,), (x_ref,), (y_ref,), diagonal)):
        left = [part[...].reshape(-1, part.shape[2]) for part in block]
        left = left[0] if len(left) == 1 else jnp.concatenate(left, axis=0)
        value = lax.dot_general(
            left, s_ref[...], (((1,), (1,)), ((), ())), preferred_element_type=F32
        ).astype(BF16)
        terms.append(jnp.dot(t_ref[k], left, preferred_element_type=F32))

        @pl.when(core == 0)
        def _():
            keep_ref[k] = value[:rows]
            send_ref[k] = value[rows:]

        @pl.when(core != 0)
        def _():
            keep_ref[k] = value[rows:]
            send_ref[k] = value[:rows]

    total = (terms[0] + terms[1]) + (terms[2] + terms[3])
    sum_ref[...] = total if len(refs) == 3 else refs[0][...] + total


def gram_chunk(core, blocks, slab, maps, running):
    rows = blocks[0].shape[1]
    total, columns = slab.shape
    out = jax.ShapeDtypeStruct((4, rows, total), BF16)
    vmem = pl.BlockSpec(memory_space=pltpu.VMEM)
    args = (*blocks, slab, maps) + (() if running is None else (running,))
    return pl.pallas_call(
        functools.partial(gram_kernel, len(blocks) - 3),
        in_specs=[pl.BlockSpec(memory_space=pltpu.SMEM)] + [vmem] * len(args),
        out_specs=[vmem] * 3,
        out_shape=[out, out, jax.ShapeDtypeStruct((maps.shape[1], columns), F32)],
        compiler_params=pltpu.CompilerParams(vmem_limit_bytes=GRAM_VMEM << 20),
        cost_estimate=pl.CostEstimate(
            flops=GRAM_FLOPS, bytes_accessed=1000, transcendentals=0
        ),
        name="gram",
    )(core, *args)


def merge_kernel(place_ref, keep_ref, recv_ref, *out_refs):
    for shift, out_ref in enumerate(out_refs):
        k = place_ref[0] ^ place_ref[1] ^ shift
        out_ref[...] = (keep_ref[k].astype(F32) + recv_ref[k].astype(F32)).astype(BF16)


def merge_chunk(place, keep, recv):
    vmem = pl.BlockSpec(memory_space=pltpu.VMEM)
    return pl.pallas_call(
        merge_kernel,
        in_specs=[pl.BlockSpec(memory_space=pltpu.SMEM), vmem, vmem],
        out_specs=[vmem] * 4,
        out_shape=[jax.ShapeDtypeStruct(keep.shape[1:], BF16)] * 4,
        compiler_params=pltpu.CompilerParams(vmem_limit_bytes=MERGE_VMEM << 20),
        cost_estimate=pl.CostEstimate(flops=1000, bytes_accessed=1000, transcendentals=0),
        name="merge",
    )(place, keep, recv)


def pairs(target):
    found = []
    for o in range(4):
        for z in range(4):
            for c in range(2):
                t = target(o, z, c)
                found.append((o * 8 + z * 2 + c, t[0] * 8 + t[1] * 2 + t[2]))
    return found


def move(value, target):
    return lax.ppermute(value, AXES, pairs(target))


def to_x(o, z, c):
    return (o ^ 1, z, c)


def to_y(o, z, c):
    return (o ^ 2, z, c)


def to_diagonal(o, z, c):
    return (o ^ 3, z, c)


def to_z1(o, z, c):
    return (o, z ^ 1, c)


def to_z2(o, z, c):
    return (o, z ^ 2, c)


def to_z3(o, z, c):
    return (o, z ^ 3, c)


def other_core(o, z, c):
    return (o, z, 1 - c)


def paired_body(p_factor, q_factor, truncation):
    own_i, bonds, columns = p_factor.shape
    bond = q_factor.shape[0]
    half_i = own_i // 2
    half_rows = half_i * bond
    total_columns = columns * lax.axis_size("inner")
    outer = lax.axis_index("outer")
    core = lax.axis_index("inner") % 2
    core_vec = core.astype(jnp.int32).reshape(1)
    place = jnp.stack([outer, lax.axis_index("inner") // 2]).astype(jnp.int32)
    p4 = p_factor.reshape(2, half_i, bonds, columns)

    slab, chunks, maps = contract(p4, q_factor, CUTS, truncation)
    maps = jnp.stack(maps).reshape(4, 2, half_rows, truncation.shape[1])
    slab = slab.reshape(2 * half_rows, columns)

    moved = []
    for t, own in enumerate(chunks):
        source = own
        if t in X_AFTER:
            source, moved[t - 1][1] = lax.optimization_barrier((own, moved[t - 1][1]))
        x = move(source, to_x)
        y = move(own, to_y)
        if t in PAIRED:
            x, y = lax.optimization_barrier((x, y))
        if ROUTES[t] == "y":
            d = move(x, to_y)
        elif ROUTES[t] == "x":
            d = move(y, to_x)
        elif ROUTES[t] == "s":
            d = (move(x[:1], to_y), move(y[1:], to_x))
        else:
            d = move(own, to_diagonal)
        moved.append([x, y, d])

    sums = []
    absorbed = None
    for t, own in enumerate(chunks):
        row0, row1 = CUTS[t] * bond, CUTS[t + 1] * bond
        for chunk, which in DUE_GRAM.get(t, ()):
            moved[t][2], moved[chunk][which] = lax.optimization_barrier((moved[t][2], moved[chunk][which]))
        if t in XY_DUE:
            moved[t][2], moved[t + 1][0], moved[t + 1][1] = lax.optimization_barrier(
                (moved[t][2], moved[t + 1][0], moved[t + 1][1])
            )
        if sums:
            due = sums[-1] if t in Z_DUE else sums[-1][:1]
            moved[t][2], *due = lax.optimization_barrier((moved[t][2], *due))
            sums[-1][: len(due)] = due
        part = maps[:, :, row0:row1].reshape(4, 2 * (row1 - row0), -1).swapaxes(1, 2)
        keep, send, absorbed = gram_chunk(core_vec, (own, *jax.tree.leaves(moved[t])), slab, part, absorbed)
        for part in Z_PARTS.get(t, ()):
            send, sums[-1][part] = lax.optimization_barrier((send, sums[-1][part]))
        for chunk, which in DUE_SEND.get(t, ()):
            send, moved[chunk][which] = lax.optimization_barrier((send, moved[chunk][which]))
        if t in XY_SEND:
            send, moved[t + 1][0], moved[t + 1][1] = lax.optimization_barrier(
                (send, moved[t + 1][0], moved[t + 1][1])
            )
        if t in D_SEND:
            send, moved[t + 1][2] = lax.optimization_barrier((send, moved[t + 1][2]))
        recv = move(send, other_core)
        pieces = merge_chunk(place, keep, recv)
        pieces = list(pieces)
        sums.append(pieces[:1] + [move(v, to) for v, to in zip(pieces[1:], (to_z1, to_z2, to_z3))])
    group = sums[-1]

    squares = jnp.full((8, 128), jnp.sum(absorbed * absorbed))
    squares = squares + move(squares, other_core)
    if GATE:
        squares, group[1] = lax.optimization_barrier((squares, group[1]))
    across = [move(squares, to) for to in (to_z1, to_z2, to_z3)]
    squares = (squares + across[0]) + (across[1] + across[2])
    sums = [sum(v.astype(F32) for v in group) for group in sums]
    gram = (jnp.concatenate(sums, axis=0) / total_columns).T
    norm_scale = jnp.sqrt(squares[:1, :1] / (absorbed.shape[0] * total_columns) + 1e-06)
    return (gram, absorbed / norm_scale)


def general_body(p_factor, q_factor, truncation):
    own_i, bonds, columns = p_factor.shape
    bond = q_factor.shape[0]
    paired = jnp.einsum("imc,jmc->ijc", p_factor, q_factor, preferred_element_type=F32)
    paired = paired / math.sqrt(bonds)
    own_rows = paired.reshape(own_i * bond, columns).astype(BF16)
    gathered = lax.all_gather(own_rows, "outer", axis=0, tiled=True)
    partial = lax.dot_general(own_rows, gathered, (((1,), (1,)), ((), ())), preferred_element_type=F32)
    total_columns = columns * lax.axis_size("inner")
    gram = lax.psum_scatter(partial, "inner", scatter_dimension=1, tiled=True) / total_columns
    local_term = lax.dot_general(truncation, own_rows, (((0,), (0,)), ((), ())), preferred_element_type=F32)
    absorbed = lax.psum(local_term, "outer")
    squares = lax.psum(jnp.sum(absorbed * absorbed), "inner")
    norm_scale = jnp.sqrt(squares / (absorbed.shape[0] * total_columns) + 1e-06)
    return (gram, absorbed / norm_scale)


def solution(mesh):
    paired = mesh.shape["outer"] == 4 and mesh.shape["inner"] == 8
    return jax.shard_map(
        paired_body if paired else general_body,
        mesh=mesh,
        in_specs=(P("outer", None, "inner"), P(None, None, "inner"), P("outer", None)),
        out_specs=(P("outer", "inner"), P(None, "inner")),
        check_vma=False,
    )
```

```python
import functools
import math

import jax
import jax.numpy as jnp
from jax import lax
from jax.experimental import pallas as pl
from jax.experimental.pallas import tpu as pltpu
from jax.sharding import PartitionSpec as P

F32 = jnp.float32
BF16 = jnp.bfloat16
AXES = ("outer", "inner")
COLUMN_TILE = 128
CUTS = (0, 2, 5, 7)
ROUTES = "yxy"
XY_DUE = ()
Z_DUE = ()
Z_PARTS = {1: (1, 2, 3), 2: (1, 2)}
XY_SEND = ()
D_SEND = (1,)
GATE = False
MAPS_AT = 1
LAST_VMEM = 52
TIE = False
X_AFTER = ()
PAIRED = (0, 1, 2)
DUE_GRAM = {}
DUE_SEND = {}
GRAM_VMEM = 20
GRAM_FLOPS = 4_000_000_000
MERGE_VMEM = 8
CONTRACT_FLOPS = 30_000_000_000


def product_rows(p_ref, q_ref, rows, cols, scale, store):
    bond = q_ref.shape[0]

    def step(group, carry):
        base = pl.multiple_of(group * 8, 8)
        q_rows = [q_ref[base + u, :, cols].astype(F32) for u in range(8)]
        for half, i in rows:
            p_row = p_ref[half, i, :, cols].astype(F32)
            sums = [jnp.sum(p_row * q_row, axis=0, keepdims=True) for q_row in q_rows]
            store(half, i, base, (jnp.concatenate(sums, axis=0) * scale).astype(BF16))
        return carry

    lax.fori_loop(0, bond // 8, step, 0)


def chunk_kernel(lo, hi, scale, p_ref, q_ref, out_ref):
    bond = q_ref.shape[0]
    rows = [(h, i) for h in range(2) for i in range(lo, hi)]
    for c in range(0, p_ref.shape[3], 128):
        cols = slice(c, c + 128)

        def store(half, i, base, value):
            out_ref[half, pl.ds((i - lo) * bond + base, 8), cols] = value

        product_rows(p_ref, q_ref, rows, cols, scale, store)


def last_kernel(cuts, scale, p_ref, q_ref, *refs):
    bond = q_ref.shape[0]
    earlier, (out_ref, slab_ref) = refs[:-2], refs[-2:]
    lo, hi = cuts[-2:]
    rows = [(h, i) for h in range(2) for i in range(lo, hi)]
    for part, ref in enumerate(earlier):
        slab_ref[:, cuts[part] * bond : cuts[part + 1] * bond, :] = ref[...]
    for c in range(0, p_ref.shape[3], 128):
        cols = slice(c, c + 128)

        def store(half, i, base, value):
            out_ref[half, pl.ds((i - lo) * bond + base, 8), cols] = value
            slab_ref[half, pl.ds(i * bond + base, 8), cols] = value

        product_rows(p_ref, q_ref, rows, cols, scale, store)


def contract(p4, q_factor, cuts, truncation):
    _, half_i, bonds, columns = p4.shape
    bond = q_factor.shape[0]
    scale = 1.0 / math.sqrt(bonds)
    tile = COLUMN_TILE

    def row_spec(rows):
        return pl.BlockSpec((2, rows, tile), lambda c: (0, 0, c))

    def row_shape(rows):
        return jax.ShapeDtypeStruct((2, rows, columns), BF16)

    factor_specs = [
        pl.BlockSpec((2, half_i, bonds, tile), lambda c: (0, 0, 0, c)),
        pl.BlockSpec((bond, bonds, tile), lambda c: (0, 0, c)),
    ]
    chunks = []
    maps = None
    if not TIE:
        maps = [truncation] + [move(truncation, to) for to in (to_x, to_y, to_diagonal)]
    for lo, hi in zip(cuts, cuts[1:]):
        last = hi == cuts[-1]
        rows = (hi - lo) * bond
        flops = 1400 * 2 * (hi - lo) * bonds * columns * bond
        earlier = chunks if last else []
        found = pl.pallas_call(
            functools.partial(last_kernel, cuts, scale) if last else functools.partial(chunk_kernel, lo, hi, scale),
            grid=(columns // tile,),
            in_specs=factor_specs + [row_spec(e.shape[1]) for e in earlier],
            out_specs=[row_spec(rows)] + ([row_spec(half_i * bond)] if last else []),
            out_shape=[row_shape(rows)] + ([row_shape(half_i * bond)] if last else []),
            compiler_params=pltpu.CompilerParams(vmem_limit_bytes=(LAST_VMEM if last else 52) << 20),
            cost_estimate=pl.CostEstimate(flops=CONTRACT_FLOPS, bytes_accessed=1000, transcendentals=0),
            name="contract",
        )(p4, q_factor, *earlier)
        own = found[0]
        if not last:
            q_factor, own = lax.optimization_barrier((q_factor, own))
            if TIE and not chunks:
                truncation, own = lax.optimization_barrier((truncation, own))
                maps = [truncation] + [move(truncation, to) for to in (to_x, to_y, to_diagonal)]
            if len(chunks) == MAPS_AT:
                q_factor, maps = lax.optimization_barrier((q_factor, maps))
        chunks.append(own)
    return found[1], chunks, maps


def gram_kernel(parts, core_ref, own_ref, x_ref, y_ref, *refs):
    diagonal, (s_ref, t_ref), refs = refs[:parts], refs[parts : parts + 2], refs[parts + 2 :]
    keep_ref, send_ref, sum_ref = refs[-3:]
    core = core_ref[0]
    rows = x_ref.shape[1]
    terms = []
    for k, block in enumerate(((own_ref,), (x_ref,), (y_ref,), diagonal)):
        left = [part[...].reshape(-1, part.shape[2]) for part in block]
        left = left[0] if len(left) == 1 else jnp.concatenate(left, axis=0)
        value = lax.dot_general(
            left, s_ref[...], (((1,), (1,)), ((), ())), preferred_element_type=F32
        ).astype(BF16)
        terms.append(jnp.dot(t_ref[k], left, preferred_element_type=F32))

        @pl.when(core == 0)
        def _():
            keep_ref[k] = value[:rows]
            send_ref[k] = value[rows:]

        @pl.when(core != 0)
        def _():
            keep_ref[k] = value[rows:]
            send_ref[k] = value[:rows]

    total = (terms[0] + terms[1]) + (terms[2] + terms[3])
    sum_ref[...] = total if len(refs) == 3 else refs[0][...] + total


def gram_chunk(core, blocks, slab, maps, running):
    rows = blocks[0].shape[1]
    total, columns = slab.shape
    out = jax.ShapeDtypeStruct((4, rows, total), BF16)
    vmem = pl.BlockSpec(memory_space=pltpu.VMEM)
    args = (*blocks, slab, maps) + (() if running is None else (running,))
    return pl.pallas_call(
        functools.partial(gram_kernel, len(blocks) - 3),
        in_specs=[pl.BlockSpec(memory_space=pltpu.SMEM)] + [vmem] * len(args),
        out_specs=[vmem] * 3,
        out_shape=[out, out, jax.ShapeDtypeStruct((maps.shape[1], columns), F32)],
        compiler_params=pltpu.CompilerParams(vmem_limit_bytes=GRAM_VMEM << 20),
        cost_estimate=pl.CostEstimate(
            flops=GRAM_FLOPS, bytes_accessed=1000, transcendentals=0
        ),
        name="gram",
    )(core, *args)


def merge_kernel(place_ref, keep_ref, recv_ref, *out_refs):
    for shift, out_ref in enumerate(out_refs):
        k = place_ref[0] ^ place_ref[1] ^ shift
        out_ref[...] = (keep_ref[k].astype(F32) + recv_ref[k].astype(F32)).astype(BF16)


def merge_chunk(place, keep, recv):
    vmem = pl.BlockSpec(memory_space=pltpu.VMEM)
    return pl.pallas_call(
        merge_kernel,
        in_specs=[pl.BlockSpec(memory_space=pltpu.SMEM), vmem, vmem],
        out_specs=[vmem] * 4,
        out_shape=[jax.ShapeDtypeStruct(keep.shape[1:], BF16)] * 4,
        compiler_params=pltpu.CompilerParams(vmem_limit_bytes=MERGE_VMEM << 20),
        cost_estimate=pl.CostEstimate(flops=1000, bytes_accessed=1000, transcendentals=0),
        name="merge",
    )(place, keep, recv)


def pairs(target):
    found = []
    for o in range(4):
        for z in range(4):
            for c in range(2):
                t = target(o, z, c)
                found.append((o * 8 + z * 2 + c, t[0] * 8 + t[1] * 2 + t[2]))
    return found


def move(value, target):
    return lax.ppermute(value, AXES, pairs(target))


def to_x(o, z, c):
    return (o ^ 1, z, c)


def to_y(o, z, c):
    return (o ^ 2, z, c)


def to_diagonal(o, z, c):
    return (o ^ 3, z, c)


def to_z1(o, z, c):
    return (o, z ^ 1, c)


def to_z2(o, z, c):
    return (o, z ^ 2, c)


def to_z3(o, z, c):
    return (o, z ^ 3, c)


def other_core(o, z, c):
    return (o, z, 1 - c)


def paired_body(p_factor, q_factor, truncation):
    own_i, bonds, columns = p_factor.shape
    bond = q_factor.shape[0]
    half_i = own_i // 2
    half_rows = half_i * bond
    total_columns = columns * lax.axis_size("inner")
    outer = lax.axis_index("outer")
    core = lax.axis_index("inner") % 2
    core_vec = core.astype(jnp.int32).reshape(1)
    place = jnp.stack([outer, lax.axis_index("inner") // 2]).astype(jnp.int32)
    p4 = p_factor.reshape(2, half_i, bonds, columns)

    slab, chunks, maps = contract(p4, q_factor, CUTS, truncation)
    maps = jnp.stack(maps).reshape(4, 2, half_rows, truncation.shape[1])
    slab = slab.reshape(2 * half_rows, columns)

    moved = []
    for t, own in enumerate(chunks):
        source = own
        if t in X_AFTER:
            source, moved[t - 1][1] = lax.optimization_barrier((own, moved[t - 1][1]))
        x = move(source, to_x)
        y = move(own, to_y)
        if t in PAIRED:
            x, y = lax.optimization_barrier((x, y))
        if ROUTES[t] == "y":
            d = move(x, to_y)
        elif ROUTES[t] == "x":
            d = move(y, to_x)
        elif ROUTES[t] == "s":
            d = (move(x[:1], to_y), move(y[1:], to_x))
        else:
            d = move(own, to_diagonal)
        moved.append([x, y, d])

    sums = []
    absorbed = None
    for t, own in enumerate(chunks):
        row0, row1 = CUTS[t] * bond, CUTS[t + 1] * bond
        for chunk, which in DUE_GRAM.get(t, ()):
            moved[t][2], moved[chunk][which] = lax.optimization_barrier((moved[t][2], moved[chunk][which]))
        if t in XY_DUE:
            moved[t][2], moved[t + 1][0], moved[t + 1][1] = lax.optimization_barrier(
                (moved[t][2], moved[t + 1][0], moved[t + 1][1])
            )
        if sums:
            due = sums[-1] if t in Z_DUE else sums[-1][:1]
            moved[t][2], *due = lax.optimization_barrier((moved[t][2], *due))
            sums[-1][: len(due)] = due
        part = maps[:, :, row0:row1].reshape(4, 2 * (row1 - row0), -1).swapaxes(1, 2)
        keep, send, absorbed = gram_chunk(core_vec, (own, *jax.tree.leaves(moved[t])), slab, part, absorbed)
        for part in Z_PARTS.get(t, ()):
            send, sums[-1][part] = lax.optimization_barrier((send, sums[-1][part]))
        for chunk, which in DUE_SEND.get(t, ()):
            send, moved[chunk][which] = lax.optimization_barrier((send, moved[chunk][which]))
        if t in XY_SEND:
            send, moved[t + 1][0], moved[t + 1][1] = lax.optimization_barrier(
                (send, moved[t + 1][0], moved[t + 1][1])
            )
        if t in D_SEND:
            send, moved[t + 1][2] = lax.optimization_barrier((send, moved[t + 1][2]))
        recv = move(send, other_core)
        pieces = merge_chunk(place, keep, recv)
        pieces = list(pieces)
        sums.append(pieces[:1] + [move(v, to) for v, to in zip(pieces[1:], (to_z1, to_z2, to_z3))])
    group = sums[-1]

    squares = jnp.full((8, 128), jnp.sum(absorbed * absorbed))
    squares = squares + move(squares, other_core)
    if GATE:
        squares, group[1] = lax.optimization_barrier((squares, group[1]))
    across = [move(squares, to) for to in (to_z1, to_z2, to_z3)]
    squares = (squares + across[0]) + (across[1] + across[2])
    sums = [sum(v.astype(F32) for v in group) for group in sums]
    gram = (jnp.concatenate(sums, axis=0) / total_columns).T
    norm_scale = jnp.sqrt(squares[:1, :1] / (absorbed.shape[0] * total_columns) + 1e-06)
    return (gram, absorbed / norm_scale)


def general_body(p_factor, q_factor, truncation):
    own_i, bonds, columns = p_factor.shape
    bond = q_factor.shape[0]
    paired = jnp.einsum("imc,jmc->ijc", p_factor, q_factor, preferred_element_type=F32)
    paired = paired / math.sqrt(bonds)
    own_rows = paired.reshape(own_i * bond, columns).astype(BF16)
    gathered = lax.all_gather(own_rows, "outer", axis=0, tiled=True)
    partial = lax.dot_general(own_rows, gathered, (((1,), (1,)), ((), ())), preferred_element_type=F32)
    total_columns = columns * lax.axis_size("inner")
    gram = lax.psum_scatter(partial, "inner", scatter_dimension=1, tiled=True) / total_columns
    local_term = lax.dot_general(truncation, own_rows, (((0,), (0,)), ((), ())), preferred_element_type=F32)
    absorbed = lax.psum(local_term, "outer")
    squares = lax.psum(jnp.sum(absorbed * absorbed), "inner")
    norm_scale = jnp.sqrt(squares / (absorbed.shape[0] * total_columns) + 1e-06)
    return (gram, absorbed / norm_scale)


def solution(mesh):
    paired = mesh.shape["outer"] == 4 and mesh.shape["inner"] == 8
    return jax.shard_map(
        paired_body if paired else general_body,
        mesh=mesh,
        in_specs=(P("outer", None, "inner"), P(None, None, "inner"), P("outer", None)),
        out_specs=(P("outer", "inner"), P(None, "inner")),
        check_vma=False,
    )
```
